32 devices in a mesh: row: 8 (over y, x, core), col: 4 (over z).
Axes of the slice: x: 2, y: 2, z: 4, core: 2. Of those that a mesh axis runs over, the one named last changes fastest.
Arguments:
- dual_ops: float32 [8, 4, 2048, 2048], P('row', 'col'), as said below
- basis: float32 [8, 4, 4, 64, 512], P('row', 'col'), may hold values from -0.125 to 0.125
- coarse_inverse: float32 [2048, 2048], P('row', 'col')
- gap_rhs: float32 [8, 4, 4, 32, 512], P('row', 'col'), may hold values from -6 to 6
- coarse_rhs: float32 [8, 4, 32, 64], P('row', 'col'), may hold values from -6 to 6
- contact_mask: int32 [8, 4, 4, 512], P('row', 'col'), may hold values 0 or 1
Outputs:
- multipliers: float32 [8, 4, 4, 32, 512], P('row', 'col')
- projected_grad: float32 [8, 4, 4, 32, 512], P('row', 'col')
The draws below stay inside these ranges and needn't reach their ends.
Inputs may be any that keep to these rules, and one draw needn't show every extreme that they name: `dual_ops`: each subdomain's dual operator is symmetric and positive definite.
All inputs are finite; a program needn't handle non-finite values. No bound on the sum of `contact_mask` on one device may be relied on, other than what follows from the above.
Results may differ from the reference program's by a relative error of at most 0.00025.
Values sent between devices are 32-bit elements; how exact they have to be, the bound alone decides.
A program may use at most 128 MiB of HBM per device.

```python
import math
import jax
import jax.numpy as jnp
from jax import lax

M = 2048
FACE = 512
K = 32
MDEV = 64
NMODES = 2048
ITERS = 6
N_ROW = 8
N_COL = 4


def draw_dual_ops(key, part):
    keys = jax.random.split(key, N_ROW * N_COL)
    limit = 4.0 / math.sqrt(M)

    def single(subkey):
        raw = jax.random.normal(subkey, (M, M), jnp.float32)
        offdiag = (raw + raw.T) * (0.5 / math.sqrt(M))
        offdiag = jnp.clip(offdiag, -limit, limit) * (1.0 - jnp.eye(M, dtype=jnp.float32))
        return offdiag + 2.5 * jnp.eye(M, dtype=jnp.float32)
    return lax.map(single, keys).reshape(N_ROW, N_COL, M, M)


def draw_coarse_inverse(key, part):
    raw = jax.random.normal(key, (NMODES, NMODES), jnp.float32)
    return jnp.eye(NMODES, dtype=jnp.float32) + raw * (0.3 / math.sqrt(NMODES))


def set_ends(values, own_key, low, high):
    place = [jax.random.randint(jax.random.fold_in(own_key, axis), (), 0, length) for axis, length in enumerate(values.shape)]
    widest = values.shape.index(max(values.shape))
    neighbour = place[:widest] + [(place[widest] + 1) % values.shape[widest]] + place[widest + 1:]
    return values.at[tuple(place)].set(low).at[tuple(neighbour)].set(high)


def level_of(stream_key, dims, cuts, low, top_value):
    def one(position, blocks):
        heights = jax.random.uniform(jax.random.fold_in(jax.random.fold_in(stream_key, 6), position), (blocks,), jnp.float32, low / len(cuts), top_value / len(cuts))
        return jnp.repeat(jnp.exp(heights), dims[position] // blocks).reshape((-1,) + (1,) * (len(dims) - position - 1))

    factor_of = one(*cuts[0])
    for cut in cuts[1:]:
        factor_of = factor_of * one(*cut)
    return factor_of


def noise(key, dims, spread, most, pieces=(), held_as=jnp.bfloat16):
    drawn = jax.random.normal(key, dims, jnp.float32) * spread
    if len(pieces) > 0:
        drawn = level_of(key, dims, pieces, -0.22, 0.18) * drawn
    return jnp.clip(drawn, min=-most, max=most).astype(held_as)


def setup_inputs(seed: int = 0) -> dict:
    splits = jax.random.split(jax.random.key(seed), 7)
    return {
        "dual_ops": draw_dual_ops(jax.random.fold_in(splits[6], 71), 0),
        "basis": noise(splits[1], (N_ROW, N_COL, 4, MDEV, FACE), M ** -0.5, 0.125, ((0, 8), (1, 4)), jnp.float32),
        "coarse_inverse": draw_coarse_inverse(jax.random.fold_in(splits[6], 71), 0),
        "gap_rhs": noise(splits[3], (N_ROW, N_COL, 4, K, FACE), 1.0, 6.0, ((0, 8), (1, 4)), jnp.float32),
        "coarse_rhs": noise(splits[4], (N_ROW, N_COL, K, MDEV), 1.0, 6.0, ((0, 8), (1, 4)), jnp.float32),
        "contact_mask": set_ends((jax.random.randint(splits[5], (N_ROW, N_COL, 4, FACE), 0, 2) < 1).astype(jnp.int32), jax.random.fold_in(splits[5], 1), 0, 1),
    }


HIGH = lax.Precision.HIGHEST


def neighbour_faces(values):
    zero_row = jnp.zeros_like(values[:1, :, 0])
    zero_col = jnp.zeros_like(values[:, :1, 0])
    from_above = jnp.concatenate([zero_row, values[:-1, :, 1]], axis=0)
    from_below = jnp.concatenate([values[1:, :, 0], zero_row], axis=0)
    from_left = jnp.concatenate([zero_col, values[:, :-1, 3]], axis=1)
    from_right = jnp.concatenate([values[:, 1:, 2], zero_col], axis=1)
    return jnp.stack([from_above, from_below, from_left, from_right], axis=2)


def interface_sum(values):
    return values + neighbour_faces(values)


def reference(dual_ops, basis, coarse_inverse, gap_rhs, coarse_rhs, contact_mask):
    blocks = dual_ops.reshape(N_ROW, N_COL, 4, FACE, 4, FACE)

    def apply_dual(vector):
        return jnp.einsum("rcgjfi,rcfki->rcgkj", blocks, vector, precision=HIGH)

    def expand(amps):
        return jnp.einsum("rcfji,rckj->rcfki", basis, amps, precision=HIGH)

    def restrict(vector):
        return jnp.einsum("rcfji,rcfki->rckj", basis, vector, precision=HIGH)

    def coarse(coef):
        column_major = jnp.transpose(coef, (2, 1, 0, 3)).reshape(K, NMODES)
        amps = jnp.dot(column_major, coarse_inverse.T, precision=HIGH, preferred_element_type=jnp.float32)
        return jnp.transpose(amps.reshape(K, N_ROW, N_COL, MDEV), (1, 2, 0, 3))

    row_ids = jnp.arange(N_ROW)[:, None]
    col_ids = jnp.arange(N_COL)[None, :]
    has_nb = jnp.stack([
        jnp.broadcast_to(row_ids > 0, (N_ROW, N_COL)),
        jnp.broadcast_to(row_ids < N_ROW - 1, (N_ROW, N_COL)),
        jnp.broadcast_to(col_ids > 0, (N_ROW, N_COL)),
        jnp.broadcast_to(col_ids < N_COL - 1, (N_ROW, N_COL))], axis=2)
    weight = jnp.where(has_nb, 0.5, 1.0).astype(jnp.float32)[:, :, :, None, None]
    contact = jnp.logical_and(contact_mask == 1, jnp.logical_not(has_nb)[:, :, :, None])[:, :, :, None, :]

    dvec = interface_sum(gap_rhs)
    multipliers = interface_sum(expand(coarse(coarse_rhs)))
    projected = jnp.zeros_like(multipliers)
    for step in range(ITERS):
        grad = interface_sum(apply_dual(multipliers)) - dvec
        projected = grad - interface_sum(expand(coarse(restrict(grad))))
        image = apply_dual(projected)
        numer = jnp.sum(weight * grad * projected, axis=(0, 1, 2, 4))
        denom = jnp.sum(projected * image, axis=(0, 1, 2, 4))
        ratio = numer / denom
        multipliers = multipliers - ratio[None, None, None, :, None] * projected
        multipliers = jnp.where(contact, jnp.maximum(multipliers, 0.0), multipliers)
    return multipliers, projected
```

```python
import functools
import math

import jax
import jax.numpy as jnp
from jax import lax
from jax.experimental import pallas as pl
from jax.experimental.pallas import tpu as pltpu
from jax.sharding import PartitionSpec as P

ITERS = 6
MESH = pl.DeviceIdType.MESH
F32 = jnp.float32
BF16 = jnp.bfloat16


def split(x):
    hi = x.astype(BF16)
    return hi, (x - hi.astype(F32)).astype(BF16)


def dot(a, b, dims):
    return lax.dot_general(a, b, (dims, ((), ())), preferred_element_type=F32)


def dot3(x, hi, lo, dims):
    rows = x.shape[0]
    x_hi, x_lo = split(x)
    both = dot(jnp.concatenate([x_hi, x_lo], axis=0), hi, dims)
    return both[:rows] + (both[rows:] + dot(x_hi, lo, dims))


def pack(x):
    half = x.shape[0] // 2
    return jnp.concatenate([x[:half], x[half:]], axis=1)


def unpack(parts):
    n = parts[0].shape[1] // 2
    top = jnp.concatenate([p[:, :n] for p in parts], axis=1)
    return jnp.concatenate([top, jnp.concatenate([p[:, n:] for p in parts], axis=1)], axis=0)


def kernel(n_rows, n_cols, a_hbm, basis, cinv, gap, crhs, mask, m_out, p_out,
           stage, ahi, alo, bhi, blo, chi, clo, nbb, nbgap, halo_in, am, dvec, grad, image, xs, whi, wlo,
           ebuf, pout, pin, amp_s, nbamps, red_a, red_b,
           a_sem, bs, br, gs, gr, hs, hr, es, er, ps, pr, ams, amr, ras, rar, rbs, rbr):
    row = lax.axis_index("row")
    col = lax.axis_index("col")
    me = row * n_cols + col
    n_dev = n_rows * n_cols
    m_len = ahi.shape[0]
    _, k, face = halo_in.shape
    mdev = nbb.shape[1]
    width = red_a.shape[2]
    step_rows = m_len // a_sem.shape[0]
    n_blocks = a_sem.shape[0]
    has_nb = [row > 0, row < n_rows - 1, col > 0, col < n_cols - 1]
    nbr = [(row - 1, col), (row + 1, col), (row, col - 1), (row, col + 1)]

    def a_copy(i):
        rows = pl.ds(pl.multiple_of(i * step_rows, step_rows), step_rows)
        return pltpu.make_async_copy(a_hbm.at[0, 0, rows], stage.at[rows], a_sem.at[i])

    def a_start(i, carry):
        a_copy(i).start()
        return carry

    lax.fori_loop(0, n_blocks, a_start, 0)

    barrier = pltpu.get_barrier_semaphore()
    for d in range(1, n_dev):
        t = lax.rem(me + d, n_dev)
        pl.semaphore_signal(barrier, inc=1, device_id=(t // n_cols, lax.rem(t, n_cols)), device_id_type=MESH)
    pl.semaphore_wait(barrier, n_dev - 1)

    def remote(src, dst, ssem, rsem, where):
        return pltpu.make_async_remote_copy(
            src_ref=src, dst_ref=dst, send_sem=ssem, recv_sem=rsem, device_id=where, device_id_type=MESH)

    def face_start(f, src, dst, ssem, rsem):
        @pl.when(has_nb[f])
        def _():
            remote(src, dst.at[f ^ 1], ssem.at[f], rsem.at[f ^ 1], nbr[f]).start()

    def face_wait(f, src, dst, ssem, rsem):
        @pl.when(has_nb[f])
        def _():
            remote(src, dst.at[f], ssem.at[f], rsem.at[f], nbr[f]).wait()

    def basis_face(f):
        return basis.at[0, 0, f]

    def coarse(use, e, first=None, second=None, third=None):
        ebuf[use, row] = pack(e)
        copies = []
        for d in range(1, n_rows):
            copies.append(remote(ebuf.at[use, row], ebuf.at[use, row], es.at[use, d], er.at[use, d], (lax.rem(row + d, n_rows), col)))
            copies[-1].start()
        if first is not None:
            first()
        for copy in copies:
            copy.wait()
        gathered = unpack([ebuf[use, r] for r in range(n_rows)])
        partial = dot3(gathered, chi[...], clo[...], ((1,), (1,)))
        for c in range(n_cols):
            pout[c] = pack(partial[:, c * mdev:(c + 1) * mdev])
        copies = []
        for d in range(1, n_cols):
            c = lax.rem(col + d, n_cols)
            copies.append(remote(pout.at[c], pin.at[use, col], ps.at[use, d], pr.at[use, d], (row, c)))
            copies[-1].start()
        pin[use, col] = pout[col]
        if second is not None:
            second()
        for copy in copies:
            copy.wait()
        amps = pin[use, 0]
        for c in range(1, n_cols):
            amps = amps + pin[use, c]
        amp_s[...] = amps
        for f in range(4):
            face_start(f, amp_s, nbamps, ams, amr)
        if third is not None:
            third()
        for f in range(4):
            face_wait(f, amp_s, nbamps, ams, amr)
        return amps

    def expand_sum(amps, f):
        both = unpack([amps, nbamps[f]])
        return dot3(both, bhi[f], blo[f], ((1,), (0,)))

    def put_split(x, f):
        hi, lo = split(x)
        xs[0:k, f * face:(f + 1) * face] = hi
        xs[k:2 * k, f * face:(f + 1) * face] = lo

    def apply_face(f):
        cols = slice(f * face, (f + 1) * face)
        both = dot(xs[...], ahi[:, cols], ((1,), (0,)))
        low = dot(xs[0:k, :], alo[:, cols], ((1,), (0,)))
        return both[:k] + (both[k:] + low)

    for f in range(4):
        face_start(f, basis_face(f), nbb, bs, br)
        face_start(f, gap.at[0, 0, f], nbgap, gs, gr)
    zero_face = jnp.zeros((k, face), F32)
    for f in range(4):
        @pl.when(jnp.logical_not(has_nb[f]))
        def _():
            nbb[f] = jnp.zeros((mdev, face), F32)
            nbgap[f] = zero_face
            halo_in[f] = zero_face
            nbamps[f] = jnp.zeros((k // 2, 2 * mdev), F32)
    c_hi, c_lo = split(cinv[...])
    chi[...] = c_hi
    clo[...] = c_lo
    for f in range(4):
        hi, lo = split(basis[0, 0, f])
        bhi[f, 0:mdev] = hi
        blo[f, 0:mdev] = lo
    amps = coarse(0, crhs[0, 0])
    for f in range(4):
        face_wait(f, basis_face(f), nbb, bs, br)
        face_wait(f, gap.at[0, 0, f], nbgap, gs, gr)
        hi, lo = split(nbb[f])
        bhi[f, mdev:2 * mdev] = hi
        blo[f, mdev:2 * mdev] = lo
        dvec[f] = gap[0, 0, f] + nbgap[f]
        m = expand_sum(amps, f)
        m_out[0, 0, f] = m
        put_split(m, f)

    def a_split(i, carry):
        a_copy(i).wait()
        rows = pl.ds(pl.multiple_of(i * step_rows, step_rows), step_rows)
        hi, lo = split(stage[rows, :])
        ahi[rows, :] = hi
        alo[rows, :] = lo
        return carry

    lax.fori_loop(0, n_blocks, a_split, 0)

    lane = lax.broadcasted_iota(jnp.int32, (k, width), 1)
    sub = lax.broadcasted_iota(jnp.int32, (k, width), 0)

    own_hi = jnp.concatenate([bhi[f, 0:mdev] for f in range(4)], axis=1)
    own_lo = jnp.concatenate([blo[f, 0:mdev] for f in range(4)], axis=1)
    own = jnp.concatenate([own_hi, own_lo], axis=0)
    for g in range(4):
        cols = slice(g * face, (g + 1) * face)
        am[g] = apply_face(g)
        both = dot(own, ahi[:, cols], ((1,), (0,)))
        low = dot(own_hi, alo[:, cols], ((1,), (0,)))
        hi, lo = split(both[:mdev] + (both[mdev:] + low))
        whi[0:mdev, cols] = hi
        wlo[0:mdev, cols] = lo
        for f in range(4):
            rows = slice(f * face, (f + 1) * face)
            nb_hi, nb_lo = bhi[f, mdev:2 * mdev], blo[f, mdev:2 * mdev]
            both = dot(jnp.concatenate([nb_hi, nb_lo], axis=0), ahi[rows, cols], ((1,), (0,)))
            low = dot(nb_hi, alo[rows, cols], ((1,), (0,)))
            hi, lo = split(both[:mdev] + (both[mdev:] + low))
            whi[(f + 1) * mdev:(f + 2) * mdev, cols] = hi
            wlo[(f + 1) * mdev:(f + 2) * mdev, cols] = lo

    def group_sum(buf, ssem, rsem, at, count, where):
        copies = []
        for d in range(1, count):
            copies.append(remote(buf.at[at], buf.at[at], ssem.at[d], rsem.at[d], where(lax.rem(at + d, count))))
            copies[-1].start()
        for copy in copies:
            copy.wait()
        return jnp.sum(buf[...], axis=0)

    def iteration(step, carry):
        for f in range(4):
            face_start(f, am.at[f], halo_in, hs, hr)
        e = jnp.zeros((k, mdev), F32)
        for f in range(4):
            face_wait(f, am.at[f], halo_in, hs, hr)
            g = am[f] + halo_in[f] - dvec[f]
            grad[f] = g
            put_split(g, f)
            e = e + dot3(g, bhi[f, 0:mdev], blo[f, 0:mdev], ((1,), (1,)))

        def first():
            image[0] = apply_face(0)
            image[1] = apply_face(1)

        def second():
            image[2] = apply_face(2)

        def third():
            image[3] = apply_face(3)

        amps = coarse(1, e, first, second, third)
        every = unpack([amps] + [nbamps[f] for f in range(4)])
        numer = jnp.zeros((k, 1), F32)
        denom = jnp.zeros((k, 1), F32)
        for f in range(4):
            cols = slice(f * face, (f + 1) * face)
            g = grad[f]
            p = g - expand_sum(amps, f)
            p_out[0, 0, f] = p
            weight = jnp.where(has_nb[f], 0.5, 1.0).astype(F32)
            numer = numer + weight * jnp.sum(g * p, axis=1, keepdims=True)
            im = image[f] - dot3(every, whi[:, cols], wlo[:, cols], ((1,), (0,)))
            image[f] = im
            denom = denom + jnp.sum(p * im, axis=1, keepdims=True)
        packed = jnp.where(lane == sub, numer, 0.0) + jnp.where(lane == sub + k, denom, 0.0)
        red_a[row] = jnp.sum(packed, axis=0, keepdims=True)
        red_b[col] = group_sum(red_a, ras, rar, row, n_rows, lambda t: (t, col))
        total = group_sum(red_b, rbs, rbr, col, n_cols, lambda t: (row, t))
        numer_all = jnp.sum(jnp.where(lane == sub, total, 0.0), axis=1, keepdims=True)
        denom_all = jnp.sum(jnp.where(lane == sub + k, total, 0.0), axis=1, keepdims=True)
        ratio = numer_all / denom_all
        for f in range(4):
            am[f] = am[f] - ratio * image[f]
            linear = m_out[0, 0, f] - ratio * p_out[0, 0, f]
            contact = jnp.where(has_nb[f], 0, mask[0, 0, f:f + 1, :])
            m = jnp.where(contact == 1, jnp.maximum(linear, 0.0), linear)
            m_out[0, 0, f] = m
            put_split(m - linear, f)
        for f in range(4):
            @pl.when(jnp.logical_and(jnp.logical_not(has_nb[f]), step < ITERS - 1))
            def _():
                rows = slice(f * face, (f + 1) * face)
                change = xs[:, rows]
                for g in range(4):
                    cols = slice(g * face, (g + 1) * face)
                    both = dot(change, ahi[rows, cols], ((1,), (0,)))
                    low = dot(change[0:k], alo[rows, cols], ((1,), (0,)))
                    am[g] = am[g] + (both[:k] + (both[k:] + low))
        return carry

    lax.fori_loop(0, ITERS, iteration, 0)


def solution(mesh):
    n_rows, n_cols = mesh.shape["row"], mesh.shape["col"]

    def shards(dual_ops, basis, coarse_inverse, gap_rhs, coarse_rhs, contact_mask):
        m_len = dual_ops.shape[-1]
        _, _, _, k, face = gap_rhs.shape
        mdev = basis.shape[3]
        width = -(-2 * k // 128) * 128
        blocks = math.gcd(m_len, 32)
        vm = pltpu.VMEM
        dma = pltpu.SemaphoreType.DMA
        small = (k // 2, 2 * mdev)
        faces = vm((4, k, face), F32)
        out = jax.ShapeDtypeStruct(gap_rhs.shape, F32)
        in_vmem = pl.BlockSpec(memory_space=pltpu.VMEM)
        return pl.pallas_call(
            functools.partial(kernel, n_rows, n_cols),
            out_shape=(out, out),
            in_specs=[pl.BlockSpec(memory_space=pl.ANY)] + [in_vmem] * 5,
            out_specs=(in_vmem, in_vmem),
            scratch_shapes=[
                vm((m_len, m_len), F32), vm((m_len, m_len), BF16), vm((m_len, m_len), BF16),
                vm((4, 2 * mdev, face), BF16), vm((4, 2 * mdev, face), BF16),
                vm(coarse_inverse.shape, BF16), vm(coarse_inverse.shape, BF16),
                vm((4, mdev, face), F32), faces, faces, faces, faces, faces, faces,
                vm((2 * k, m_len), BF16), vm((5 * mdev, m_len), BF16), vm((5 * mdev, m_len), BF16),
                vm((2, n_rows, *small), F32), vm((n_cols, *small), F32), vm((2, n_cols, *small), F32),
                vm(small, F32), vm((4, *small), F32), vm((n_rows, 1, width), F32), vm((n_cols, 1, width), F32),
                dma((blocks,)),
                dma((4,)), dma((4,)), dma((4,)), dma((4,)), dma((4,)), dma((4,)),
                dma((2, n_rows)), dma((2, n_rows)), dma((2, n_cols)), dma((2, n_cols)),
                dma((4,)), dma((4,)), dma((n_rows,)), dma((n_rows,)), dma((n_cols,)), dma((n_cols,)),
            ],
            compiler_params=pltpu.CompilerParams(
                collective_id=0, has_side_effects=True, vmem_limit_bytes=60 * 1024 * 1024),
        )(dual_ops, basis, coarse_inverse, gap_rhs, coarse_rhs, contact_mask)

    return jax.shard_map(
        shards,
        mesh=mesh,
        in_specs=(
            P("row", "col", None, None),
            P("row", "col", None, None, None),
            P("row", "col"),
            P("row", "col", None, None, None),
            P("row", "col", None, None),
            P("row", "col", None, None),
        ),
        out_specs=(P("row", "col", None, None, None), P("row", "col", None, None, None)),
        check_vma=False,
    )
```
